128 devices in a mesh: wide: 16 (over y, x), narrow: 8 (over z, core).
Axes of the slice: x: 4, y: 4, z: 4, core: 2. Of those that a mesh axis runs over, the one named last changes fastest.
Arguments:
- tokens: bfloat16 [256, 128, 1536], P('wide'), may hold values from -8 to 8
- ln_gain: bfloat16 [1536], replicated, may hold values from 0.3984375 to 1.59375
- gate_weight: bfloat16 [1536, 8960], P(None, 'narrow'), may hold values from -0.15625 to 0.15625
- up_weight: bfloat16 [1536, 8960], P(None, 'narrow'), may hold values from -0.15625 to 0.15625
- down_weight: bfloat16 [8960, 1536], P('narrow'), may hold values from -0.0625 to 0.0625
- out_gain: bfloat16 [1536], replicated, may hold values from 0.25 to 1.75
- shard_ids: int32 [256], P('wide'), may hold values from 0 to 15, as said below
- slab_old: bfloat16 [262144, 1536], P(('wide', 'narrow')), may hold values from -8 to 8
- queries: bfloat16 [16, 64, 1536], P('wide'), may hold values from -12 to 12
- positives: int32 [16, 64], P('wide'), may hold values from 0 to 262399
- owners: int32 [4], replicated, may hold values from 0 to 15
Outputs:
- index_new: bfloat16 [16, 16, 2, 1536], P('wide', 'narrow')
- losses: float32 [4, 64], replicated
The draws below stay inside these ranges and needn't reach their ends.
Inputs may be any that keep to these rules, and one draw needn't show every extreme that they name: `shard_ids`: among the 16 passages of one index of wide at most 2 have the same shard id; in every draw one shard id is held by exactly 2 passages of every index of wide.
All inputs are finite; a program needn't handle non-finite values.
Results may differ from the reference program's by a relative error of at most 0.0029.
Values may be sent and summed in bfloat16 or wider, within the bound.
No kernel may reach another device: no remote copies, remote signals or barrier semaphores. Data moves between devices by JAX's collectives and lax.ppermute only.
A program may use at most 128 MiB of HBM per device.

```python
import math
import jax
import jax.numpy as jnp
from jax import lax

D = 1536
FF = 8960
SEQ = 128
PASS = 16
QB = 64
STEPS = 4
CAP = 2
NEW_TOTAL = 256
OLD_TOTAL = 262144
N_WIDE = 16


def block_patterns(key):
    return jnp.where(jax.random.bernoulli(jax.random.fold_in(key, 9), 0.5, (N_WIDE, D)), 1.0, -1.0).astype(jnp.float32)


def draw_tokens(key, part):
    k_topic = jax.random.fold_in(key, 21)
    k_noise = jax.random.fold_in(key, 22)
    k_jitter = jax.random.fold_in(key, 24)
    k_place = jax.random.fold_in(key, 10)
    columns = jnp.arange(D, dtype=jnp.float32) / D
    patterns = block_patterns(key)
    ramp = 0.8 + 0.6 * columns
    topic = jax.random.normal(k_topic, (NEW_TOTAL, 1, D), jnp.float32)
    noise = jax.random.normal(k_noise, (NEW_TOTAL, SEQ, D), jnp.float32)
    values = topic * ramp + noise
    jitter = 0.3 * jax.random.normal(k_jitter, (N_WIDE, SEQ, D), jnp.float32)
    planted = 2.0 * patterns[:, None, :] + jitter
    chosen = jax.random.randint(k_place, (N_WIDE,), 0, PASS)
    marked = (jnp.arange(PASS, dtype=jnp.int32)[None, :] == chosen[:, None])[:, :, None, None]
    values = jnp.where(marked, planted[:, None, :, :], values.reshape(N_WIDE, PASS, SEQ, D))
    return jnp.clip(values, -8.0, 8.0).reshape(NEW_TOTAL, SEQ, D).astype(jnp.bfloat16)


def draw_shard_ids(key, part):
    full = jax.random.randint(jax.random.fold_in(key, 3), (), 0, N_WIDE)
    others = jnp.arange((N_WIDE - 1) * CAP, dtype=jnp.int32) // CAP
    others = others + (others >= full).astype(jnp.int32)
    keys = jax.random.split(jax.random.fold_in(key, 4), N_WIDE)

    def block(block_key):
        first_key, second_key = jax.random.split(block_key)
        chosen = jax.random.permutation(first_key, others)[:PASS - CAP]
        rows = jnp.concatenate([jnp.full((CAP,), full, jnp.int32), chosen])
        return jax.random.permutation(second_key, rows)
    return jax.vmap(block)(keys).reshape(NEW_TOTAL).astype(jnp.int32)


def draw_slab_old(key, part):
    k_base = jax.random.fold_in(key, 11)
    rows = jnp.arange(OLD_TOTAL, dtype=jnp.float32) / OLD_TOTAL
    ramp = (0.94 + 0.12 * rows)[:, None]
    values = jax.random.normal(k_base, (OLD_TOTAL, D), jnp.float32) * ramp
    return jnp.clip(values, -8.0, 8.0).astype(jnp.bfloat16)


def draw_queries(key, part):
    k_base = jax.random.fold_in(key, 31)
    row_ids = jnp.arange(N_WIDE * QB, dtype=jnp.int32)
    patterns = block_patterns(key)
    matched = patterns[row_ids // 8 % N_WIDE] * 4.0
    to_new = (row_ids % 8 == 4)[:, None]
    values = jax.random.normal(k_base, (N_WIDE * QB, D), jnp.float32) * 6.0
    values = jnp.where(to_new, matched, values)
    return jnp.clip(values, -12.0, 12.0).reshape(N_WIDE, QB, D).astype(jnp.bfloat16)


def touch_ends(array, rng, smallest, high):
    spot = [jax.random.randint(jax.random.fold_in(rng, axis), (), 0, length) for axis, length in enumerate(array.shape)]
    widest = array.shape.index(max(array.shape))
    next_to = spot[:widest] + [(spot[widest] + 1) % array.shape[widest]] + spot[widest + 1:]
    return array.at[tuple(spot)].set(smallest).at[tuple(next_to)].set(high)


def block_levels(rng, shape, cuts, smallest, high):
    loudness, own = 1.0, jax.random.fold_in(rng, 6)
    for dim, shards_of in cuts:
        steps = jnp.exp(jax.random.uniform(jax.random.fold_in(own, dim), (shards_of,), jnp.float32, smallest / len(cuts), high / len(cuts)))
        loudness = loudness * jnp.repeat(steps, shape[dim] // shards_of).reshape([-1 if axis == dim else 1 for axis in range(len(shape))])
    return loudness


def bell_draw(own_key, extent, deviation, limit, cuts=(), kind=jnp.bfloat16):
    drawn = deviation * jax.random.normal(own_key, extent, jnp.float32)
    if cuts:
        drawn = drawn * block_levels(own_key, extent, cuts, -0.22, 0.18)
    return jnp.clip(drawn, -limit, limit).astype(kind)


def setup_inputs(seed: int = 0) -> dict:
    streams_of = jax.random.split(jax.random.key(seed), 12)
    tokens = draw_tokens(jax.random.fold_in(streams_of[11], 71), 0)
    ln_gain = jnp.clip(1.0 + 0.12 * jax.random.normal(streams_of[1], (D,), jnp.float32), 0.3984375, 1.59375).astype(jnp.bfloat16)
    gate_weight = bell_draw(streams_of[2], (D, FF), D ** -0.5, 0.15625, ((1, 8),))
    up_weight = bell_draw(streams_of[3], (D, FF), D ** -0.5, 0.15625, ((1, 8),))
    down_weight = bell_draw(streams_of[4], (FF, D), FF ** -0.5, 0.0625, ((0, 8),))
    out_gain = jnp.clip(1.0 + 0.15 * jax.random.normal(streams_of[5], (D,), jnp.float32), 0.25, 1.75).astype(jnp.bfloat16)
    shard_ids = draw_shard_ids(jax.random.fold_in(streams_of[11], 71), 0)
    slab_old = draw_slab_old(jax.random.fold_in(streams_of[11], 71), 0)
    queries = draw_queries(jax.random.fold_in(streams_of[11], 71), 0)
    positives = touch_ends(jax.random.randint(streams_of[9], (N_WIDE, QB), 0, OLD_TOTAL + NEW_TOTAL), jax.random.fold_in(streams_of[9], 1), 0, (OLD_TOTAL + NEW_TOTAL) - 1).astype(jnp.int32)
    owners = touch_ends(jax.random.randint(streams_of[10], (STEPS,), 0, N_WIDE), jax.random.fold_in(streams_of[10], 1), 0, N_WIDE - 1).astype(jnp.int32)
    return {"tokens": tokens, "ln_gain": ln_gain, "gate_weight": gate_weight, "up_weight": up_weight, "down_weight": down_weight, "out_gain": out_gain, "shard_ids": shard_ids, "slab_old": slab_old, "queries": queries, "positives": positives, "owners": owners}


EPS = 1e-06

def rms_scale(values):
    return lax.rsqrt(lax.optimization_barrier(jnp.mean(values * values, axis=-1, keepdims=True)) + EPS)

def reference(tokens, ln_gain, gate_weight, up_weight, down_weight, out_gain, shard_ids, slab_old, queries, positives, owners):
    gain_in = ln_gain.astype(jnp.float32)
    gain_out = out_gain.astype(jnp.float32)

    def encode(group):
        values = group.astype(jnp.float32)
        normed = (values * rms_scale(values) * gain_in).astype(jnp.bfloat16).reshape(PASS * SEQ, D)
        gate = jnp.dot(normed, gate_weight, preferred_element_type=jnp.float32)
        upward = jnp.dot(normed, up_weight, preferred_element_type=jnp.float32)
        hidden = (jax.nn.silu(gate) * upward).astype(jnp.bfloat16)
        mixed = jnp.dot(hidden, down_weight, preferred_element_type=jnp.float32).reshape(PASS, SEQ, D)
        pooled = lax.optimization_barrier(jnp.mean(values + mixed, axis=1))
        return (pooled * rms_scale(pooled) * gain_out).astype(jnp.bfloat16)
    embeddings = lax.map(encode, tokens.reshape(N_WIDE, PASS, SEQ, D))
    positions = jnp.arange(PASS, dtype=jnp.int32)
    earlier = positions[:, None] > positions[None, :]

    def place(shards, rows):
        same = shards[:, None] == shards[None, :]
        rank = lax.optimization_barrier(jnp.sum((earlier & same).astype(jnp.int32), axis=1))
        slots = (shards * CAP + rank).astype(jnp.int32)
        empty = jnp.zeros((N_WIDE * CAP, D), jnp.bfloat16)
        return empty.at[slots].set(rows).reshape(N_WIDE, CAP, D)
    placed = jax.vmap(place)(shard_ids.reshape(N_WIDE, PASS), embeddings)
    index_new = jnp.transpose(placed, (1, 0, 2, 3))
    fresh = embeddings.reshape(NEW_TOTAL, D)
    scale = 1.0 / math.sqrt(D)
    contract = (((1,), (1,)), ((), ()))

    def step_loss(owner):
        block = queries[owner]
        positive = positives[owner]
        old_scores = lax.dot_general(block, slab_old, contract, preferred_element_type=jnp.float32) * scale
        new_scores = lax.dot_general(block, fresh, contract, preferred_element_type=jnp.float32) * scale
        scores = jnp.concatenate([old_scores, new_scores], axis=1)
        top = lax.optimization_barrier(jnp.max(scores, axis=1))
        total = lax.optimization_barrier(jnp.sum(jnp.exp(scores - top[:, None]), axis=1))
        picked = jnp.take_along_axis(scores, positive[:, None].astype(jnp.int32), axis=1)[:, 0]
        return top + jnp.log(total) - picked
    losses = lax.map(step_loss, owners)
    return (index_new, losses)
```

```python
import functools
import math

import jax
import jax.numpy as jnp
from jax import lax
from jax.experimental import pallas as pl
from jax.experimental.pallas import tpu as pltpu
from jax.sharding import PartitionSpec as P

EPS = 1e-06

f32, bf16, i32 = jnp.float32, jnp.bfloat16, jnp.int32
NT = (((1,), (1,)), ((), ()))
NN = (((1,), (0,)), ((), ()))
VMEM = pl.BlockSpec(memory_space=pltpu.VMEM)
SMEM = pl.BlockSpec(memory_space=pltpu.SMEM)
ANY = pl.BlockSpec(memory_space=pl.ANY)

SIDE = 4
PIECES = 4


def dot(a, b, dims):
    return lax.dot_general(a, b, dims, preferred_element_type=f32)


def split3(v):
    high = v.astype(bf16)
    rest = v - high.astype(f32)
    middle = rest.astype(bf16)
    low = (rest - middle.astype(f32)).astype(bf16)
    return high, middle, low


def rms_scale(values):
    return lax.rsqrt(jnp.mean(values * values, axis=-1, keepdims=True) + EPS)


def encode_kernel(tok_ref, gain_ref, wg_ref, wu_ref, *rest):
    hm_ref, tm_ref = rest[-2:]
    count, seq, width = tok_ref.shape
    units = wg_ref.shape[0]
    values = tok_ref[...].reshape(count * seq, width).astype(f32)
    normed = (values * rms_scale(values) * gain_ref[...].astype(f32)).astype(bf16)
    tm_ref[0] = jnp.mean(values.reshape(count, seq, width), axis=1)

    def pooled(gate, up):
        hidden = (gate / (1.0 + jnp.exp(-gate)) * up).astype(bf16).astype(f32)
        return jnp.mean(hidden.reshape(count, seq, hidden.shape[1]), axis=1)

    for lo in range(0, units, 128):
        hi = min(lo + 128, units)
        both = jnp.concatenate([wg_ref[lo:hi, :], wu_ref[lo:hi, :]], axis=0)
        if hi - lo == 128:
            out = dot(normed, both, NT)
            gate, up = out[:, :128], out[:, 128:]
        else:
            gate = dot(normed, wg_ref[lo:hi, :], NT)
            up = dot(normed, wu_ref[lo:hi, :], NT)
        hm_ref[0, :, lo:hi] = pooled(gate, up)


def encode(piece, tokens, gain, wg, wu, after):
    passages, seq, width = tokens.shape
    count = passages // PIECES
    units = wg.shape[0]
    return pl.pallas_call(
        encode_kernel,
        grid=(1,),
        in_specs=[
            pl.BlockSpec((count, seq, width), lambda i: (piece, 0, 0)),
            pl.BlockSpec((1, width), lambda i: (0, 0)),
            VMEM,
            VMEM,
        ]
        + [ANY] * len(after),
        out_specs=[
            pl.BlockSpec((1, count, units), lambda i: (0, 0, 0)),
            pl.BlockSpec((1, count, width), lambda i: (0, 0, 0)),
        ],
        out_shape=[
            jax.ShapeDtypeStruct((1, count, units), f32),
            jax.ShapeDtypeStruct((1, count, width), f32),
        ],
        cost_estimate=pl.CostEstimate(
            flops=4 * count * seq * width * units,
            transcendentals=count * seq * units,
            bytes_accessed=2 * (count * seq + 2 * units) * width,
        ),
        name=f"encode{piece}",
    )(tokens, gain, wg, wu, *after)


def down_kernel(where_ref, ids_ref, down_ref, *rest):
    hms, tms = rest[:PIECES], rest[PIECES : 2 * PIECES]
    keep_ref, send_ref, place_ref = rest[2 * PIECES :]
    hm = jnp.concatenate([r[0] for r in hms], axis=0)
    tm = jnp.concatenate([r[0] for r in tms], axis=0)
    rows = hm.shape[0]
    parts = jnp.concatenate(split3(hm), axis=0)
    out = dot(parts, down_ref[...], NN)
    part = out[:rows] + (out[rows : 2 * rows] + out[2 * rows :])
    narrow = where_ref[0] * 2 + where_ref[1]
    row = lax.broadcasted_iota(i32, part.shape, 0)
    part = part + jnp.where(row // 2 == narrow, tm, 0.0)
    half = rows // 2
    low, high = part[:half], part[half:]
    first = where_ref[1] == 0
    keep_ref[...] = jnp.where(first, low, high)
    send_ref[...] = jnp.where(first, high, low)
    ids = jnp.broadcast_to(ids_ref[...], (128, 128)).astype(f32)
    column = jnp.transpose(ids)
    sub = lax.broadcasted_iota(i32, (128, 128), 0)
    lane = lax.broadcasted_iota(i32, (128, 128), 1)
    same = (ids == column) & (sub < lane) & (sub < rows)
    rank = jnp.sum(jnp.where(same, 1.0, 0.0), axis=0, keepdims=True)
    slot = lax.broadcasted_iota(i32, (32, 128), 0)
    ids32 = jnp.broadcast_to(ids_ref[...], (32, 128))
    hit = (ids32 == slot % 16) & (rank.astype(i32) == slot // 16)
    hit = hit & (lax.broadcasted_iota(i32, (32, 128), 1) < rows)
    place_ref[...] = jnp.where(hit, 1.0, 0.0).astype(bf16)


def score_kernel(scale, where_ref, own_ref, other_ref, slab_ref, stats_ref, q_ref):
    step = pl.program_id(0)
    block, width = slab_ref.shape
    chunk = own_ref.shape[1]
    z, core = where_ref[0], where_ref[1]

    @pl.when(step == 0)
    def _():
        for k in range(SIDE):
            layer = lax.rem(z + SIDE - k, SIDE)
            mine = pl.multiple_of((layer * 2 + core) * chunk, chunk)
            theirs = pl.multiple_of((layer * 2 + 1 - core) * chunk, chunk)
            q_ref[pl.ds(mine, chunk), :] = own_ref[k]
            q_ref[pl.ds(theirs, chunk), :] = other_ref[k]
        row = lax.broadcasted_iota(i32, stats_ref.shape, 0)
        stats_ref[...] = jnp.where(row == 0, -jnp.inf, 0.0)

    scores = dot(slab_ref[...], q_ref[:, :width], NT) * scale
    target = positive_row(q_ref, width) - (where_ref[2] + step * block)
    row = lax.broadcasted_iota(i32, scores.shape, 0)
    old_max, total = stats_ref[0:1, :], stats_ref[1:2, :]
    new_max = jnp.maximum(old_max, jnp.max(scores, axis=0, keepdims=True))
    stats_ref[1:2, :] = total * jnp.exp(old_max - new_max) + jnp.sum(
        jnp.exp(scores - new_max), axis=0, keepdims=True
    )
    stats_ref[0:1, :] = new_max
    stats_ref[2:3, :] += jnp.sum(jnp.where(row == target, scores, 0.0), axis=0, keepdims=True)


def positive_row(q_ref, width):
    lane = lax.broadcasted_iota(i32, (8, 128), 1)
    weight = jnp.where(lane == 0, 65536.0, jnp.where(lane == 1, 256.0, 1.0))
    weight = jnp.where(lane < 3, weight, 0.0).astype(bf16)
    return dot(weight, q_ref[:, width:], NT)[0:1].astype(i32)


def score(where, own, other, slab, scale):
    rows, width = slab.shape
    block = 512
    queries = 2 * own.shape[0] * own.shape[1]
    return pl.pallas_call(
        functools.partial(score_kernel, scale),
        grid=(rows // block,),
        in_specs=[SMEM, VMEM, VMEM, pl.BlockSpec((block, width), lambda i: (i, 0))],
        out_specs=[
            pl.BlockSpec((8, queries), lambda i: (0, 0)),
            pl.BlockSpec((queries, own.shape[2]), lambda i: (0, 0)),
        ],
        out_shape=[
            jax.ShapeDtypeStruct((8, queries), f32),
            jax.ShapeDtypeStruct((queries, own.shape[2]), bf16),
        ],
        cost_estimate=pl.CostEstimate(
            flops=2 * rows * width * queries,
            transcendentals=rows * queries,
            bytes_accessed=2 * rows * width,
        ),
        name="score",
    )(where, own, other, slab)


def merge(parts):
    top = functools.reduce(jnp.maximum, [p[0] for p in parts])
    total = sum(p[1] * jnp.exp(p[0] - top) for p in parts)
    picked = sum(p[2] for p in parts)
    return top, total, picked


def stats_of(row, base, count):
    return tuple(row[:, base + i * count : base + (i + 1) * count] for i in range(3))


def pack_kernel(keep_ref, got_ref, stats_ref, out_ref):
    width, count = keep_ref.shape[1], stats_ref.shape[1]
    out_ref[:, :width] = keep_ref[...] + got_ref[...]
    out_ref[:, width:] = jnp.zeros((8, 3 * count), f32)
    for i in range(3):
        out_ref[0:1, width + i * count : width + (i + 1) * count] = stats_ref[i : i + 1, :]


def embed_kernel(scale, old_total, where_ref, gain_ref, q_ref, *rest):
    ins, out_ref, layers_ref = rest[:SIDE], rest[SIDE], rest[SIDE + 1]
    width = gain_ref.shape[1]
    count = q_ref.shape[0]
    z, core, wide = where_ref[0], where_ref[1], where_ref[3]
    for k in range(SIDE):
        layers_ref[lax.rem(z + SIDE - k, SIDE)] = ins[k][...]
    layers = [layers_ref[k] for k in range(SIDE)]
    pooled = (layers[0][:, :width] + layers[1][:, :width]) + (
        layers[2][:, :width] + layers[3][:, :width]
    )
    emb = (pooled * rms_scale(pooled) * gain_ref[...].astype(f32)).astype(bf16)
    scores = dot(emb, q_ref[:, :width], NT) * scale
    target = positive_row(q_ref, width)
    number = old_total + wide * 16 + core * 8 + lax.broadcasted_iota(i32, scores.shape, 0)
    top = jnp.max(scores, axis=0, keepdims=True)
    total = jnp.sum(jnp.exp(scores - top), axis=0, keepdims=True)
    picked = jnp.sum(jnp.where(number == target, scores, 0.0), axis=0, keepdims=True)
    olds = [stats_of(layer[0:1], width, count) for layer in layers]
    stats = merge(olds + [(top, total, picked)])
    out_ref[:, :width] = emb.astype(f32)
    out_ref[:, width:] = jnp.zeros((8, 3 * count), f32)
    for i in range(3):
        out_ref[0:1, width + i * count : width + (i + 1) * count] = stats[i]


def dispatch_kernel(where_ref, place_ref, mine_ref, other_ref, out_ref):
    width = mine_ref.shape[1] * 2 // 3
    count = (mine_ref.shape[1] - width) // 3
    first = where_ref[1] == 0
    mine, other = mine_ref[:, :width], other_ref[:, :width]
    emb = jnp.concatenate([jnp.where(first, mine, other), jnp.where(first, other, mine)], axis=0)
    slots = dot(place_ref[:, :16], emb.astype(bf16), NN)
    stats = merge([stats_of(r[0:1, :], width, count) for r in (mine_ref, other_ref)])
    stats = jnp.concatenate(stats, axis=1)
    out_ref[:, 0, :width] = slots[:16]
    out_ref[:, 0, width : 2 * width] = slots[16:]
    out_ref[:, 0, 2 * width :] = jnp.broadcast_to(stats, (16, 3 * count))


def finish_kernel(where_ref, got_ref, index_ref, loss_ref):
    width = index_ref.shape[-1]
    count = (got_ref.shape[-1] - 2 * width) // 3
    narrow = where_ref[0] * 2 + where_ref[1]
    for source in range(2):
        row = got_ref[2 * narrow + source]
        index_ref[0, source, 0:1, :] = row[:, :width].astype(bf16)
        index_ref[0, source, 1:2, :] = row[:, width : 2 * width].astype(bf16)
    stats = got_ref[:, 0, 2 * width :]
    tops, totals, picks = stats_of(stats, 0, count)
    top = jnp.max(tops, axis=0, keepdims=True)
    total = jnp.sum(totals * jnp.exp(tops - top), axis=0, keepdims=True)
    loss = top + jnp.log(total) - jnp.sum(picks, axis=0, keepdims=True)
    lane = lax.broadcasted_iota(i32, (8, count), 1)
    sub = lax.broadcasted_iota(i32, (8, count), 0)
    masked = jnp.where((lane // 8) % 4 == sub, loss, 0.0)
    row = lax.broadcasted_iota(i32, (count, 128), 0)
    column = lax.broadcasted_iota(i32, (count, 128), 1)
    pick = (row // 32 == column // 8) & (row % 8 == column % 8)
    pick = jnp.where(pick, 1.0, 0.0).astype(bf16)
    high, middle, low = (dot(v, pick, NN) for v in split3(masked))
    loss_ref[...] = ((high + middle) + low)[0:4, 0:64]


def shift_x(value, k):
    return lax.ppermute(value, "wide", [(i, i // 4 * 4 + (i + k) % 4) for i in range(16)])


def shift_y(value, k):
    return lax.ppermute(value, "wide", [(i, (i + 4 * k) % 16) for i in range(16)])


def shift_z(value, k):
    return lax.ppermute(value, "narrow", [(i, (i + 2 * k) % 8) for i in range(8)])


def swap_core(value):
    return lax.ppermute(value, "narrow", [(i, i ^ 1) for i in range(8)])


def pick(index, choices):
    out = choices[-1]
    for k in range(len(choices) - 2, -1, -1):
        out = jnp.where(index == k, choices[k], out)
    return out


def local(
    tokens,
    ln_gain,
    gate_weight,
    up_weight,
    down_weight,
    out_gain,
    shard_ids,
    slab_old,
    queries,
    positives,
    owners,
):
    width = tokens.shape[2]
    narrow, wide = lax.axis_index("narrow"), lax.axis_index("wide")
    x, y = wide % SIDE, wide // SIDE
    z, core = narrow // 2, narrow % 2
    old_total = slab_old.shape[0] * lax.axis_size("narrow") * lax.axis_size("wide")
    base = (wide * lax.axis_size("narrow") + narrow) * slab_old.shape[0]
    where = jnp.stack([z, core, base, wide]).astype(i32)
    scale = 1.0 / math.sqrt(width)
    steps = owners.shape[0]

    mine = lax.dynamic_slice_in_dim(queries[0], narrow * 8, 8, 0)
    number = lax.dynamic_slice_in_dim(positives[0], narrow * 8, 8, 0)[:, None]
    lane = lax.broadcasted_iota(i32, (8, 128), 1)
    digits = jnp.where(lane == 0, number >> 16, jnp.where(lane == 1, (number >> 8) & 255, number & 255))
    digits = jnp.where(lane < 3, digits, 0).astype(bf16)
    mine = jnp.concatenate([mine, digits], axis=1)

    gain = ln_gain[None]
    wg, wu = gate_weight.T, up_weight.T
    hms, tms = [], []

    def piece(index, after):
        hm, tm = encode(index, tokens, gain, wg, wu, after)
        hms.append(hm)
        tms.append(tm)

    with jax.named_scope("query_x"):
        rows = [mine] + [shift_x(mine, k) for k in range(1, SIDE)]
    piece(0, [])
    held = jnp.stack([pick((x + SIDE - owners[t] % SIDE) % SIDE, rows) for t in range(steps)])
    with jax.named_scope("query_y"):
        planes = [held] + [shift_y(held, k) for k in range(1, SIDE)]
    piece(1, rows[1:])
    held = jnp.stack(
        [pick((y + SIDE - owners[t] // SIDE) % SIDE, [p[t] for p in planes]) for t in range(steps)]
    ).reshape(steps * 8, -1)
    with jax.named_scope("query_z"):
        layers = jnp.stack([held] + [shift_z(held, k) for k in range(1, SIDE)])
    piece(2, planes[1:])
    with jax.named_scope("query_core"):
        other = swap_core(layers)
    piece(3, [layers])

    ids = jnp.pad(shard_ids, (0, 112))[None]
    half = jax.ShapeDtypeStruct((8, width), f32)
    keep, send, place = pl.pallas_call(
        down_kernel,
        in_specs=[SMEM, VMEM, VMEM] + [VMEM] * (2 * PIECES),
        out_specs=[VMEM] * 3,
        out_shape=[half, half, jax.ShapeDtypeStruct((32, 128), bf16)],
        name="down",
    )(where, ids, down_weight, *hms, *tms)
    with jax.named_scope("sum_core"):
        got = swap_core(send)
    stats, q = score(where, layers, other, slab_old, scale)
    packed = jax.ShapeDtypeStruct((8, width + 3 * q.shape[0]), f32)
    summed = pl.pallas_call(
        pack_kernel,
        in_specs=[VMEM] * 3,
        out_specs=VMEM,
        out_shape=packed,
        name="pack",
    )(keep, got, stats)
    with jax.named_scope("sum_z"):
        parts = [summed] + [shift_z(summed, k) for k in range(1, SIDE)]
    embedded = pl.pallas_call(
        functools.partial(embed_kernel, scale, old_total),
        in_specs=[SMEM] + [VMEM] * (2 + SIDE),
        out_specs=VMEM,
        out_shape=packed,
        scratch_shapes=[pltpu.VMEM((SIDE,) + packed.shape, f32)],
        name="embed",
    )(where, out_gain[None], q, *parts)
    with jax.named_scope("embed_core"):
        partner = swap_core(embedded)
    outgoing = pl.pallas_call(
        dispatch_kernel,
        in_specs=[SMEM] + [VMEM] * 3,
        out_specs=VMEM,
        out_shape=jax.ShapeDtypeStruct((16, 1, 2 * width + 3 * q.shape[0]), f32),
        name="dispatch",
    )(where, place, embedded, partner)
    arrived = lax.all_to_all(outgoing, "wide", split_axis=0, concat_axis=0, tiled=True)
    return tuple(
        pl.pallas_call(
            finish_kernel,
            in_specs=[SMEM, VMEM],
            out_specs=[VMEM] * 2,
            out_shape=[
                jax.ShapeDtypeStruct((1, 2, 2, width), bf16),
                jax.ShapeDtypeStruct((steps, 64), f32),
            ],
            name="finish",
        )(where, arrived)
    )


def solution(mesh):
    return jax.shard_map(
        local,
        mesh=mesh,
        in_specs=(
            P("wide", None, None),
            P(),
            P(None, "narrow"),
            P(None, "narrow"),
            P("narrow", None),
            P(),
            P("wide"),
            P(("wide", "narrow"), None),
            P("wide", None, None),
            P("wide", None),
            P(),
        ),
        out_specs=(P("wide", "narrow", None, None), P()),
        check_vma=False,
    )
```

```python
import functools
import math

import jax
import jax.numpy as jnp
from jax import lax
from jax.experimental import pallas as pl
from jax.experimental.pallas import tpu as pltpu
from jax.sharding import PartitionSpec as P

EPS = 1e-06

f32, bf16, i32 = jnp.float32, jnp.bfloat16, jnp.int32
NT = (((1,), (1,)), ((), ()))
NN = (((1,), (0,)), ((), ()))
VMEM = pl.BlockSpec(memory_space=pltpu.VMEM)
SMEM = pl.BlockSpec(memory_space=pltpu.SMEM)
ANY = pl.BlockSpec(memory_space=pl.ANY)
HBM = pl.BlockSpec(memory_space=pltpu.HBM)

FRONT_FLOPS = 10 * 10**9
PICK_FLOPS = 5 * 10**9
SIDE = 4
BLOCK = 4


def dot(a, b, dims):
    return lax.dot_general(a, b, dims, preferred_element_type=f32)


def split3(v):
    high = v.astype(bf16)
    rest = v - high.astype(f32)
    middle = rest.astype(bf16)
    low = (rest - middle.astype(f32)).astype(bf16)
    return high, middle, low


def rms_scale(values):
    return lax.rsqrt(jnp.mean(values * values, axis=-1, keepdims=True) + EPS)


def encode_kernel(
    where_ref,
    ids_ref,
    gain_ref,
    tok_hbm,
    wg_hbm,
    wu_hbm,
    down_hbm,
    keep_ref,
    send_ref,
    place_ref,
    hm_ref,
    tm_ref,
    tok_ref,
    w_ref,
    down_ref,
    tok_sem,
    w_sem,
    down_sem,
):
    blocks, count, units = hm_ref.shape
    seq, width = tok_hbm.shape[1:]
    tiles = w_ref.shape[0]
    gain = gain_ref[...].reshape(1, width).astype(f32)

    def fetch(b):
        slot = b % 2
        return pltpu.make_async_copy(
            tok_hbm.at[pl.ds(b * count, count)], tok_ref.at[slot], tok_sem.at[slot]
        )

    weights = []
    for j in range(tiles):
        size = min(128, units - 128 * j)
        for i, hbm in enumerate((wg_hbm, wu_hbm)):
            source = hbm.at[pl.ds(128 * j, size)]
            target = w_ref.at[j, pl.ds(128 * i, size)]
            weights.append(pltpu.make_async_copy(source, target, w_sem.at[j, i]))

    def block(b, wait):
        values = tok_ref[b % 2].reshape(count * seq, width).astype(f32)
        normed = (values * rms_scale(values) * gain).astype(bf16)
        tm_ref[b] = jnp.mean(values.reshape(count, seq, width), axis=1)
        if wait:
            for copy in wait[:-2]:
                copy.wait()
            for copy in wait[-2:]:
                copy.start()
        for j in range(tiles):
            out = dot(normed, w_ref[j], NT)
            gate, up = out[:, :128], out[:, 128:]
            hidden = (gate / (1.0 + jnp.exp(-gate)) * up).astype(bf16).astype(f32)
            mean = jnp.mean(hidden.reshape(count, seq, 128), axis=1)
            size = min(128, units - 128 * j)
            hm_ref[b, :, 128 * j : 128 * j + size] = mean[:, :size]

    fetch(0).start()
    for copy in weights:
        copy.start()
    fetch(0).wait()
    down = pltpu.make_async_copy(down_hbm, down_ref, down_sem)
    block(0, weights + [fetch(1), down])

    @pl.loop(1, blocks)
    def _(b):
        @pl.when(b + 1 < blocks)
        def _():
            fetch(b + 1).start()

        fetch(b).wait()
        block(b, [])

    down.wait()
    finish_pooled(where_ref, ids_ref, down_ref, hm_ref, tm_ref, keep_ref, send_ref, place_ref)


def encode(where, ids, gain, tokens, wg, wu, down):
    passages, seq, width = tokens.shape
    blocks = passages // BLOCK
    units = wg.shape[0]
    tiles = -(-units // 128)
    large = [pltpu.with_memory_space_constraint(v, pltpu.HBM) for v in (tokens, wg, wu, down)]
    half = jax.ShapeDtypeStruct((passages // 2, width), f32)
    return pl.pallas_call(
        encode_kernel,
        in_specs=[SMEM, VMEM, VMEM] + [HBM] * 4,
        out_specs=[VMEM] * 3,
        out_shape=[half, half, jax.ShapeDtypeStruct((32, 128), bf16)],
        scratch_shapes=[
            pltpu.VMEM((blocks, BLOCK, units), f32),
            pltpu.VMEM((blocks, BLOCK, width), f32),
            pltpu.VMEM((2, BLOCK, seq, width), bf16),
            pltpu.VMEM((tiles, 256, width), bf16),
            pltpu.VMEM(down.shape, bf16),
            pltpu.SemaphoreType.DMA((2,)),
            pltpu.SemaphoreType.DMA((tiles, 2)),
            pltpu.SemaphoreType.DMA,
        ],
        cost_estimate=pl.CostEstimate(
            flops=4 * passages * seq * width * units,
            transcendentals=passages * seq * units,
            bytes_accessed=2 * (passages * seq + 3 * units) * width,
        ),
        compiler_params=pltpu.CompilerParams(vmem_limit_bytes=28 << 20),
        name="encode",
    )(where, ids, gain, *large)


def finish_pooled(where_ref, ids_ref, down_ref, hm_ref, tm_ref, keep_ref, send_ref, place_ref):
    hm = jnp.concatenate([hm_ref[i] for i in range(hm_ref.shape[0])], axis=0)
    tm = jnp.concatenate([tm_ref[i] for i in range(tm_ref.shape[0])], axis=0)
    rows = hm.shape[0]
    parts = jnp.concatenate(split3(hm), axis=0)
    out = dot(parts, down_ref[...], NN)
    part = out[:rows] + (out[rows : 2 * rows] + out[2 * rows :])
    narrow = where_ref[0] * 2 + where_ref[1]
    row = lax.broadcasted_iota(i32, part.shape, 0)
    part = part + jnp.where(row // 2 == narrow, tm, 0.0)
    half = rows // 2
    low, high = part[:half], part[half:]
    first = where_ref[1] == 0
    keep_ref[...] = jnp.where(first, low, high)
    send_ref[...] = jnp.where(first, high, low)
    id_row = jnp.concatenate([ids_ref[...].reshape(1, rows), jnp.zeros((1, 128 - rows), i32)], axis=1)
    ids = jnp.broadcast_to(id_row, (128, 128)).astype(f32)
    column = jnp.transpose(ids)
    sub = lax.broadcasted_iota(i32, (128, 128), 0)
    lane = lax.broadcasted_iota(i32, (128, 128), 1)
    same = (ids == column) & (sub < lane) & (sub < rows)
    rank = jnp.sum(jnp.where(same, 1.0, 0.0), axis=0, keepdims=True)
    slot = lax.broadcasted_iota(i32, (32, 128), 0)
    ids32 = jnp.broadcast_to(id_row, (32, 128))
    hit = (ids32 == slot % 16) & (rank.astype(i32) == slot // 16)
    hit = hit & (lax.broadcasted_iota(i32, (32, 128), 1) < rows)
    place_ref[...] = jnp.where(hit, 1.0, 0.0).astype(bf16)


def front_kernel(core_ref, query_ref, positive_ref, out_ref, digit_ref):
    copies, rows = out_ref.shape[:2]
    width = query_ref.shape[2]
    number = jnp.concatenate(
        [positive_ref[...], jnp.zeros((1, 128 - positive_ref.shape[1]), i32)], axis=1
    )
    sub = lax.broadcasted_iota(i32, (128, 128), 0)
    digits = jnp.where(sub == 0, number >> 16, jnp.where(sub == 1, (number >> 8) & 255, number & 255))
    digit_ref[...] = jnp.transpose(jnp.where(sub < 3, digits, 0).astype(f32))
    own = digit_ref[pl.ds(pl.multiple_of(core_ref[0] * rows, rows), rows), :].astype(bf16)
    for w in range(copies):
        out_ref[w, :, :width] = query_ref[0]
        out_ref[w, :, width:] = own


def front(core, queries, positives, copies):
    queries, positives = (
        pltpu.with_memory_space_constraint(v, pltpu.HBM) for v in (queries, positives)
    )
    size, width = queries.shape[1:]
    rows = size // 2
    shape = jax.ShapeDtypeStruct((copies, rows, width + 128), bf16)
    return pl.pallas_call(
        front_kernel,
        grid_spec=pltpu.PrefetchScalarGridSpec(
            num_scalar_prefetch=1,
            grid=(1,),
            in_specs=[
                pl.BlockSpec((1, rows, width), lambda i, c: (0, c[0], 0)),
                pl.BlockSpec((1, size), lambda i, c: (0, 0)),
            ],
            out_specs=pl.BlockSpec(shape.shape, lambda i, c: (0, 0, 0)),
            scratch_shapes=[pltpu.VMEM((128, 128), f32)],
        ),
        out_shape=shape,
        cost_estimate=pl.CostEstimate(flops=FRONT_FLOPS, transcendentals=0, bytes_accessed=2 << 20),
        compiler_params=pltpu.CompilerParams(vmem_limit_bytes=8 << 20),
        name="front",
    )(core, queries, positives)


def pick_kernel(owners_ref, got_ref, after_ref, out_ref):
    size = got_ref.shape[1]
    for t in range(out_ref.shape[0] // size):
        out_ref[t * size : (t + 1) * size, :] = got_ref[owners_ref[t]]


def score_kernel(scale, where_ref, own_ref, other_ref, slab_ref, stats_ref, q_ref):
    step = pl.program_id(0)
    block, width = slab_ref.shape
    half = own_ref.shape[0]

    @pl.when(step == 0)
    def _():
        core = where_ref[1]
        q_ref[pl.ds(pl.multiple_of(core * half, half), half), :] = own_ref[...]
        q_ref[pl.ds(pl.multiple_of((1 - core) * half, half), half), :] = other_ref[...]
        row = lax.broadcasted_iota(i32, stats_ref.shape, 0)
        stats_ref[...] = jnp.where(row == 0, -jnp.inf, 0.0)

    target = positive_row(q_ref, width) - (where_ref[2] + step * block)
    parts = [tuple(stats_ref[i : i + 1, :] for i in range(3))]
    for lo in range(0, block, 256):
        scores = dot(slab_ref[lo : lo + 256, :], q_ref[:, :width], NT) * scale
        row = lax.broadcasted_iota(i32, scores.shape, 0) + lo
        top = jnp.max(scores, axis=0, keepdims=True)
        total = jnp.sum(jnp.exp(scores - top), axis=0, keepdims=True)
        picked = jnp.sum(jnp.where(row == target, scores, 0.0), axis=0, keepdims=True)
        parts.append((top, total, picked))
    for i, value in enumerate(merge(parts)):
        stats_ref[i : i + 1, :] = value


def positive_row(q_ref, width):
    lane = lax.broadcasted_iota(i32, (8, 128), 1)
    weight = jnp.where(lane == 0, 65536.0, jnp.where(lane == 1, 256.0, 1.0))
    weight = jnp.where(lane < 3, weight, 0.0).astype(bf16)
    return dot(weight, q_ref[:, width:], NT)[0:1].astype(i32)


def score(where, own, other, slab, scale):
    rows, width = slab.shape
    block = 1024
    queries = 2 * own.shape[0]
    return pl.pallas_call(
        functools.partial(score_kernel, scale),
        grid=(rows // block,),
        in_specs=[SMEM, VMEM, VMEM, pl.BlockSpec((block, width), lambda i: (i, 0))],
        out_specs=[
            pl.BlockSpec((8, queries), lambda i: (0, 0)),
            pl.BlockSpec((queries, own.shape[1]), lambda i: (0, 0)),
        ],
        out_shape=[
            jax.ShapeDtypeStruct((8, queries), f32),
            jax.ShapeDtypeStruct((queries, own.shape[1]), bf16),
        ],
        cost_estimate=pl.CostEstimate(
            flops=2 * rows * width * queries,
            transcendentals=rows * queries,
            bytes_accessed=2 * rows * width,
        ),
        compiler_params=pltpu.CompilerParams(vmem_limit_bytes=16 << 20),
        name="score",
    )(where, own, other, slab)


def merge(parts):
    top = functools.reduce(jnp.maximum, [p[0] for p in parts])
    total = sum(p[1] * jnp.exp(p[0] - top) for p in parts)
    picked = sum(p[2] for p in parts)
    return top, total, picked


def stats_of(row, base, count):
    return tuple(row[:, base + i * count : base + (i + 1) * count] for i in range(3))


def put_stats(ref, width, stats):
    flat = jnp.concatenate(stats, axis=1)
    rows = flat.shape[1] // 128
    for i in range(ref.shape[0]):
        lanes = flat[:, i * 128 : (i + 1) * 128] if i < rows else jnp.zeros((1, 128), f32)
        ref[i : i + 1, width:] = lanes


def get_stats(value, width, count):
    flat = jnp.concatenate([value[i : i + 1, width:] for i in range(3 * count // 128)], axis=1)
    return stats_of(flat, 0, count)


def pack_kernel(keep_ref, got_ref, stats_ref, out_ref):
    width = keep_ref.shape[1]
    out_ref[:, :width] = keep_ref[...] + got_ref[...]
    put_stats(out_ref, width, [stats_ref[i : i + 1, :] for i in range(3)])


def embed_kernel(scale, old_total, where_ref, gain_ref, q_ref, *rest):
    ins, out_ref, layers_ref = rest[:SIDE], rest[SIDE], rest[SIDE + 1]
    width = gain_ref.shape[0]
    count = q_ref.shape[0]
    z, core, wide = where_ref[0], where_ref[1], where_ref[3]
    for k in range(SIDE):
        layers_ref[lax.rem(z + SIDE - k, SIDE)] = ins[k][...]
    layers = [layers_ref[k] for k in range(SIDE)]
    pooled = (layers[0][:, :width] + layers[1][:, :width]) + (
        layers[2][:, :width] + layers[3][:, :width]
    )
    gain = gain_ref[...].reshape(1, width).astype(f32)
    emb = (pooled * rms_scale(pooled) * gain).astype(bf16)
    scores = dot(emb, q_ref[:, :width], NT) * scale
    target = positive_row(q_ref, width)
    number = old_total + wide * 16 + core * 8 + lax.broadcasted_iota(i32, scores.shape, 0)
    top = jnp.max(scores, axis=0, keepdims=True)
    total = jnp.sum(jnp.exp(scores - top), axis=0, keepdims=True)
    picked = jnp.sum(jnp.where(number == target, scores, 0.0), axis=0, keepdims=True)
    olds = [get_stats(layer, width, count) for layer in layers]
    stats = merge(olds + [(top, total, picked)])
    out_ref[:, :width] = emb.astype(f32)
    put_stats(out_ref, width, stats)


def dispatch_kernel(where_ref, place_ref, mine_ref, other_ref, out_ref):
    width = mine_ref.shape[1] - 128
    count = (out_ref.shape[2] - width) // 3
    first = where_ref[1] == 0
    mine, other = mine_ref[:, :width], other_ref[:, :width]
    emb = jnp.concatenate([jnp.where(first, mine, other), jnp.where(first, other, mine)], axis=0)
    slots = dot(place_ref[:, :16], emb.astype(bf16), NN)
    top, total, picked = merge([get_stats(r[...], width, count) for r in (mine_ref, other_ref)])
    tails = [jnp.concatenate(split3(v), axis=1) for v in (top + jnp.log(total), picked)]
    for shard in range(16):
        for c in range(2):
            at = c * 16 + shard
            out_ref[shard, c : c + 1, :width] = slots[at : at + 1].astype(bf16)
            out_ref[shard, c : c + 1, width:] = tails[c]


def finish_kernel(where_ref, got_ref, index_ref, loss_ref):
    width = index_ref.shape[-1]
    count = (got_ref.shape[-1] - width) // 3
    narrow = where_ref[0] * 2 + where_ref[1]
    for source in range(2):
        index_ref[0, source] = got_ref[2 * narrow + source, :, :width]

    def whole(c):
        rows = [got_ref[w, c : c + 1, width:].astype(f32) for w in range(got_ref.shape[0])]
        rows = jnp.concatenate(rows, axis=0)
        high, middle, low = (rows[:, i * count : (i + 1) * count] for i in range(3))
        return (high + middle) + low

    parts, picks = whole(0), whole(1)
    top = jnp.max(parts, axis=0, keepdims=True)
    total = jnp.sum(jnp.exp(parts - top), axis=0, keepdims=True)
    loss = top + jnp.log(total) - jnp.sum(picks, axis=0, keepdims=True)
    lane = lax.broadcasted_iota(i32, (8, count), 1)
    sub = lax.broadcasted_iota(i32, (8, count), 0)
    masked = jnp.where((lane // 32) % 4 == sub, loss, 0.0)
    row = lax.broadcasted_iota(i32, (count, 128), 0)
    column = lax.broadcasted_iota(i32, (count, 128), 1)
    pick = (row // 128 == column // 32) & (row % 32 == column % 32)
    pick = jnp.where(pick, 1.0, 0.0).astype(bf16)
    high, middle, low = (dot(v, pick, NN) for v in split3(masked))
    loss_ref[...] = ((high + middle) + low)[0:4, 0:64]


def shift_z(value, k):
    return lax.ppermute(value, "narrow", [(i, (i + 2 * k) % 8) for i in range(8)])


def swap_core(value):
    return lax.ppermute(value, "narrow", [(i, i ^ 1) for i in range(8)])


def local(
    tokens,
    ln_gain,
    gate_weight,
    up_weight,
    down_weight,
    out_gain,
    shard_ids,
    slab_old,
    queries,
    positives,
    owners,
):
    width = tokens.shape[2]
    narrow, wide = lax.axis_index("narrow"), lax.axis_index("wide")
    z, core = (narrow >> 1).astype(i32), (narrow & 1).astype(i32)
    narrow_count, wide_count = lax.axis_size("narrow"), lax.axis_size("wide")
    old_total = slab_old.shape[0] * narrow_count * wide_count
    base = (wide * narrow_count + narrow) * slab_old.shape[0]
    where = jnp.stack([z, core, base, wide]).astype(i32)
    scale = 1.0 / math.sqrt(width)
    small = pltpu.CompilerParams(vmem_limit_bytes=16 << 20)
    steps = owners.shape[0]

    wg, wu = gate_weight.T, up_weight.T
    with jax.named_scope("query_wide"):
        got = front(core.reshape(1), queries, positives, wide_count)
        got = lax.all_to_all(got, "wide", split_axis=0, concat_axis=0, tiled=True)
    keep, send, place = encode(where, shard_ids, ln_gain, tokens, wg, wu, down_weight)
    with jax.named_scope("sum_core"):
        arrived = swap_core(send)
    own = pl.pallas_call(
        pick_kernel,
        in_specs=[SMEM, VMEM, ANY],
        out_specs=VMEM,
        out_shape=jax.ShapeDtypeStruct((steps * got.shape[1], got.shape[2]), bf16),
        cost_estimate=pl.CostEstimate(
            flops=PICK_FLOPS, transcendentals=0, bytes_accessed=got.size * 2
        ),
        compiler_params=small,
        name="pick",
    )(owners, got, keep)
    with jax.named_scope("query_core"):
        other = swap_core(own)

    stats, q = score(where, own, other, slab_old, scale)
    packed = jax.ShapeDtypeStruct((8, width + 128), f32)
    summed = pl.pallas_call(
        pack_kernel,
        in_specs=[VMEM] * 3,
        out_specs=VMEM,
        out_shape=packed,
        compiler_params=small,
        name="pack",
    )(keep, arrived, stats)
    with jax.named_scope("sum_z"):
        parts = [summed] + [shift_z(summed, k) for k in range(1, SIDE)]
    embedded = pl.pallas_call(
        functools.partial(embed_kernel, scale, old_total),
        in_specs=[SMEM] + [VMEM] * (2 + SIDE),
        out_specs=VMEM,
        out_shape=packed,
        scratch_shapes=[pltpu.VMEM((SIDE,) + packed.shape, f32)],
        compiler_params=small,
        name="embed",
    )(where, out_gain, q, *parts)
    with jax.named_scope("embed_core"):
        partner = swap_core(embedded)
    outgoing = pl.pallas_call(
        dispatch_kernel,
        in_specs=[SMEM] + [VMEM] * 3,
        out_specs=VMEM,
        out_shape=jax.ShapeDtypeStruct((16, 2, width + 3 * q.shape[0]), bf16),
        compiler_params=small,
        name="dispatch",
    )(where, place, embedded, partner)
    arrived = lax.all_to_all(outgoing, "wide", split_axis=0, concat_axis=0, tiled=True)
    return tuple(
        pl.pallas_call(
            finish_kernel,
            in_specs=[SMEM, VMEM],
            out_specs=[VMEM] * 2,
            out_shape=[
                jax.ShapeDtypeStruct((1, 2, 2, width), bf16),
                jax.ShapeDtypeStruct((steps, 64), f32),
            ],
            compiler_params=small,
        name="finish",
        )(where, arrived)
    )


def solution(mesh):
    return jax.shard_map(
        local,
        mesh=mesh,
        in_specs=(
            P("wide", None, None),
            P(),
            P(None, "narrow"),
            P(None, "narrow"),
            P("narrow", None),
            P(),
            P("wide"),
            P(("wide", "narrow"), None),
            P("wide", None, None),
            P("wide", None),
            P(),
        ),
        out_specs=(P("wide", "narrow", None, None), P()),
        check_vma=False,
    )
```

```python
import functools
import math

import jax
import jax.numpy as jnp
from jax import lax
from jax.experimental import pallas as pl
from jax.experimental.pallas import tpu as pltpu
from jax.sharding import PartitionSpec as P

EPS = 1e-06

f32, bf16, i32 = jnp.float32, jnp.bfloat16, jnp.int32
NT = (((1,), (1,)), ((), ()))
NN = (((1,), (0,)), ((), ()))
VMEM = pl.BlockSpec(memory_space=pltpu.VMEM)
SMEM = pl.BlockSpec(memory_space=pltpu.SMEM)
ANY = pl.BlockSpec(memory_space=pl.ANY)
HBM = pl.BlockSpec(memory_space=pltpu.HBM)

SCORE_BLOCK = 1024
FRONT_FLOPS = 10 * 10**9
PICK_FLOPS = 5 * 10**9
SIDE = 4
BLOCK = 4


def dot(a, b, dims):
    return lax.dot_general(a, b, dims, preferred_element_type=f32)


def split3(v):
    high = v.astype(bf16)
    rest = v - high.astype(f32)
    middle = rest.astype(bf16)
    low = (rest - middle.astype(f32)).astype(bf16)
    return high, middle, low


def rms_scale(values):
    return lax.rsqrt(jnp.mean(values * values, axis=-1, keepdims=True) + EPS)


def encode_kernel(
    where_ref,
    ids_ref,
    gain_ref,
    tok_hbm,
    wg_hbm,
    wu_hbm,
    down_hbm,
    keep_ref,
    send_ref,
    place_ref,
    hm_ref,
    tm_ref,
    tok_ref,
    w_ref,
    down_ref,
    tok_sem,
    w_sem,
    down_sem,
):
    blocks, count, units = hm_ref.shape
    seq, width = tok_hbm.shape[1:]
    tiles = w_ref.shape[0]
    gain = gain_ref[...].reshape(1, width).astype(f32)

    def fetch(b):
        slot = b % 2
        return pltpu.make_async_copy(
            tok_hbm.at[pl.ds(b * count, count)], tok_ref.at[slot], tok_sem.at[slot]
        )

    weights = []
    for j in range(tiles):
        size = min(128, units - 128 * j)
        for i, hbm in enumerate((wg_hbm, wu_hbm)):
            source = hbm.at[pl.ds(128 * j, size)]
            target = w_ref.at[j, pl.ds(128 * i, size)]
            weights.append(pltpu.make_async_copy(source, target, w_sem.at[j, i]))

    def block(b, wait):
        values = tok_ref[b % 2].reshape(count * seq, width).astype(f32)
        normed = (values * rms_scale(values) * gain).astype(bf16)
        tm_ref[b] = jnp.mean(values.reshape(count, seq, width), axis=1)
        if wait:
            for copy in wait[:-2]:
                copy.wait()
            for copy in wait[-2:]:
                copy.start()
        for j in range(tiles):
            out = dot(normed, w_ref[j], NT)
            gate, up = out[:, :128], out[:, 128:]
            hidden = (gate / (1.0 + jnp.exp(-gate)) * up).astype(bf16).astype(f32)
            mean = jnp.mean(hidden.reshape(count, seq, 128), axis=1)
            size = min(128, units - 128 * j)
            hm_ref[b, :, 128 * j : 128 * j + size] = mean[:, :size]

    fetch(0).start()
    for copy in weights:
        copy.start()
    fetch(0).wait()
    down = pltpu.make_async_copy(down_hbm, down_ref, down_sem)
    block(0, weights + [fetch(1), down])

    @pl.loop(1, blocks)
    def _(b):
        @pl.when(b + 1 < blocks)
        def _():
            fetch(b + 1).start()

        fetch(b).wait()
        block(b, [])

    down.wait()
    finish_pooled(where_ref, ids_ref, down_ref, hm_ref, tm_ref, keep_ref, send_ref, place_ref)


def encode(where, ids, gain, tokens, wg, wu, down):
    passages, seq, width = tokens.shape
    blocks = passages // BLOCK
    units = wg.shape[0]
    tiles = -(-units // 128)
    large = [pltpu.with_memory_space_constraint(v, pltpu.HBM) for v in (tokens, wg, wu, down)]
    half = jax.ShapeDtypeStruct((passages // 2, width), f32)
    return pl.pallas_call(
        encode_kernel,
        in_specs=[SMEM, VMEM, VMEM] + [HBM] * 4,
        out_specs=[VMEM] * 3,
        out_shape=[half, half, jax.ShapeDtypeStruct((32, 128), bf16)],
        scratch_shapes=[
            pltpu.VMEM((blocks, BLOCK, units), f32),
            pltpu.VMEM((blocks, BLOCK, width), f32),
            pltpu.VMEM((2, BLOCK, seq, width), bf16),
            pltpu.VMEM((tiles, 256, width), bf16),
            pltpu.VMEM(down.shape, bf16),
            pltpu.SemaphoreType.DMA((2,)),
            pltpu.SemaphoreType.DMA((tiles, 2)),
            pltpu.SemaphoreType.DMA,
        ],
        cost_estimate=pl.CostEstimate(
            flops=4 * passages * seq * width * units,
            transcendentals=passages * seq * units,
            bytes_accessed=2 * (passages * seq + 3 * units) * width,
        ),
        compiler_params=pltpu.CompilerParams(vmem_limit_bytes=28 << 20),
        name="encode",
    )(where, ids, gain, *large)


def finish_pooled(where_ref, ids_ref, down_ref, hm_ref, tm_ref, keep_ref, send_ref, place_ref):
    hm = jnp.concatenate([hm_ref[i] for i in range(hm_ref.shape[0])], axis=0)
    tm = jnp.concatenate([tm_ref[i] for i in range(tm_ref.shape[0])], axis=0)
    rows = hm.shape[0]
    parts = jnp.concatenate(split3(hm), axis=0)
    out = dot(parts, down_ref[...], NN)
    part = out[:rows] + (out[rows : 2 * rows] + out[2 * rows :])
    narrow = where_ref[0] * 2 + where_ref[1]
    row = lax.broadcasted_iota(i32, part.shape, 0)
    part = part + jnp.where(row // 2 == narrow, tm, 0.0)
    half = rows // 2
    low, high = part[:half], part[half:]
    first = where_ref[1] == 0
    keep_ref[...] = jnp.where(first, low, high)
    send_ref[...] = jnp.where(first, high, low)
    id_row = jnp.concatenate([ids_ref[...].reshape(1, rows), jnp.zeros((1, 128 - rows), i32)], axis=1)
    ids = jnp.broadcast_to(id_row, (128, 128)).astype(f32)
    column = jnp.transpose(ids)
    sub = lax.broadcasted_iota(i32, (128, 128), 0)
    lane = lax.broadcasted_iota(i32, (128, 128), 1)
    same = (ids == column) & (sub < lane) & (sub < rows)
    rank = jnp.sum(jnp.where(same, 1.0, 0.0), axis=0, keepdims=True)
    slot = lax.broadcasted_iota(i32, (32, 128), 0)
    ids32 = jnp.broadcast_to(id_row, (32, 128))
    hit = (ids32 == slot % 16) & (rank.astype(i32) == slot // 16)
    hit = hit & (lax.broadcasted_iota(i32, (32, 128), 1) < rows)
    place_ref[...] = jnp.where(hit, 1.0, 0.0).astype(bf16)


def front_kernel(core_ref, query_ref, positive_ref, out_ref):
    rows, width = query_ref.shape[1:]
    spare = out_ref.shape[1] - rows * width // 128
    first = core_ref[0] == 0
    number = jnp.where(first, positive_ref[:, :rows], positive_ref[:, rows:])
    number = jnp.concatenate([number, jnp.zeros((1, 128 - rows), i32)], axis=1)
    sub = lax.broadcasted_iota(i32, (spare, 128), 0)
    digits = jnp.where(sub == 0, number >> 16, jnp.where(sub == 1, (number >> 8) & 255, number & 255))
    digits = jnp.where(sub < 3, digits, 0).astype(f32).astype(bf16)
    for w in range(out_ref.shape[0]):
        for j in range(width // 128):
            out_ref[w, j * rows : (j + 1) * rows, :] = query_ref[0, :, j * 128 : (j + 1) * 128]
        out_ref[w, rows * width // 128 :, :] = digits


def front(core, queries, positives, copies):
    size, width = queries.shape[1:]
    rows = size // 2
    queries, positives = (
        pltpu.with_memory_space_constraint(v, pltpu.HBM) for v in (queries, positives)
    )
    shape = jax.ShapeDtypeStruct((copies, rows * width // 128 + 8, 128), bf16)
    return pl.pallas_call(
        front_kernel,
        grid_spec=pltpu.PrefetchScalarGridSpec(
            num_scalar_prefetch=1,
            grid=(1,),
            in_specs=[
                pl.BlockSpec((1, rows, width), lambda i, c: (0, c[0], 0)),
                pl.BlockSpec((1, size), lambda i, c: (0, 0)),
            ],
            out_specs=pl.BlockSpec(shape.shape, lambda i, c: (0, 0, 0)),
        ),
        out_shape=shape,
        cost_estimate=pl.CostEstimate(flops=FRONT_FLOPS, transcendentals=0, bytes_accessed=2 << 20),
        compiler_params=pltpu.CompilerParams(vmem_limit_bytes=8 << 20),
        name="front",
    )(core, queries, positives)


def pick_kernel(owners_ref, got_ref, after_ref, out_ref):
    width = out_ref.shape[1] - 128
    tiles = width // 128
    rows = (got_ref.shape[1] - 8) // tiles
    unit = lax.broadcasted_iota(i32, (rows, 128), 0) == lax.broadcasted_iota(i32, (rows, 128), 1)
    unit = jnp.where(unit, 1.0, 0.0).astype(bf16)
    for t in range(out_ref.shape[0] // rows):
        owner = owners_ref[t]
        at = slice(t * rows, (t + 1) * rows)
        for j in range(tiles):
            out_ref[at, j * 128 : (j + 1) * 128] = got_ref[owner, j * rows : (j + 1) * rows, :]
        digits = got_ref[owner, tiles * rows :, :].astype(f32)
        digits = jnp.concatenate([digits, jnp.zeros((120, 128), f32)], axis=0).astype(bf16)
        out_ref[at, width:] = dot(unit, digits, NT).astype(bf16)


def score_kernel(scale, where_ref, own_ref, other_ref, slab_hbm, stats_ref, q_ref, slab_ref, sem):
    chunks, block, width = slab_ref.shape
    half = own_ref.shape[0]
    copies = [
        pltpu.make_async_copy(slab_hbm.at[pl.ds(i * block, block)], slab_ref.at[i], sem.at[i])
        for i in range(chunks)
    ]
    copies[0].start()
    core = where_ref[1]
    q_ref[pl.ds(pl.multiple_of(core * half, half), half), :] = own_ref[...]
    q_ref[pl.ds(pl.multiple_of((1 - core) * half, half), half), :] = other_ref[...]
    target = positive_row(q_ref, width) - where_ref[2]
    found = []
    for i in range(chunks):
        copies[i].wait()
        if i == 0:
            for copy in copies[1:]:
                copy.start()
        for lo in range(0, block, 256):
            scores = dot(slab_ref[i, lo : lo + 256, :], q_ref[:, :width], NT) * scale
            row = lax.broadcasted_iota(i32, scores.shape, 0) + (i * block + lo)
            top = jnp.max(scores, axis=0, keepdims=True)
            total = jnp.sum(jnp.exp(scores - top), axis=0, keepdims=True)
            picked = jnp.sum(jnp.where(row == target, scores, 0.0), axis=0, keepdims=True)
            found.append((top, total, picked))
    stats_ref[...] = jnp.zeros(stats_ref.shape, f32)
    for i, value in enumerate(merge(found)):
        stats_ref[i : i + 1, :] = value


def positive_row(q_ref, width):
    lane = lax.broadcasted_iota(i32, (8, 128), 1)
    weight = jnp.where(lane == 0, 65536.0, jnp.where(lane == 1, 256.0, 1.0))
    weight = jnp.where(lane < 3, weight, 0.0).astype(bf16)
    return dot(weight, q_ref[:, width:], NT)[0:1].astype(i32)


def score(where, own, other, slab, scale):
    rows, width = slab.shape
    queries, lanes = 2 * own.shape[0], own.shape[1]
    return pl.pallas_call(
        functools.partial(score_kernel, scale),
        in_specs=[SMEM, VMEM, VMEM, HBM],
        out_specs=[VMEM] * 2,
        out_shape=[
            jax.ShapeDtypeStruct((8, queries), f32),
            jax.ShapeDtypeStruct((queries, lanes), bf16),
        ],
        scratch_shapes=[
            pltpu.VMEM((rows // SCORE_BLOCK, SCORE_BLOCK, width), bf16),
            pltpu.SemaphoreType.DMA((rows // SCORE_BLOCK,)),
        ],
        cost_estimate=pl.CostEstimate(
            flops=2 * rows * width * queries,
            transcendentals=rows * queries,
            bytes_accessed=2 * rows * width,
        ),
        compiler_params=pltpu.CompilerParams(vmem_limit_bytes=16 << 20),
        name="score",
    )(where, own, other, pltpu.with_memory_space_constraint(slab, pltpu.HBM))


def merge(parts):
    top = functools.reduce(jnp.maximum, [p[0] for p in parts])
    total = sum(p[1] * jnp.exp(p[0] - top) for p in parts)
    picked = sum(p[2] for p in parts)
    return top, total, picked


def stats_of(row, base, count):
    return tuple(row[:, base + i * count : base + (i + 1) * count] for i in range(3))


def put_stats(ref, width, stats):
    flat = jnp.concatenate(stats, axis=1)
    rows = flat.shape[1] // 128
    for i in range(ref.shape[0]):
        lanes = flat[:, i * 128 : (i + 1) * 128] if i < rows else jnp.zeros((1, 128), f32)
        ref[i : i + 1, width:] = lanes


def get_stats(value, width, count):
    flat = jnp.concatenate([value[i : i + 1, width:] for i in range(3 * count // 128)], axis=1)
    return stats_of(flat, 0, count)


def pack_kernel(keep_ref, got_ref, stats_ref, out_ref):
    width = keep_ref.shape[1]
    out_ref[:, :width] = keep_ref[...] + got_ref[...]
    put_stats(out_ref, width, [stats_ref[i : i + 1, :] for i in range(3)])


def embed_kernel(scale, old_total, where_ref, gain_ref, q_ref, *rest):
    ins, out_ref, layers_ref = rest[:SIDE], rest[SIDE], rest[SIDE + 1]
    width = gain_ref.shape[0]
    count = q_ref.shape[0]
    z, core, wide = where_ref[0], where_ref[1], where_ref[3]
    for k in range(SIDE):
        layers_ref[lax.bitwise_xor(z, k)] = ins[k][...]
    layers = [layers_ref[k] for k in range(SIDE)]
    pooled = (layers[0][:, :width] + layers[1][:, :width]) + (
        layers[2][:, :width] + layers[3][:, :width]
    )
    gain = gain_ref[...].reshape(1, width).astype(f32)
    emb = (pooled * rms_scale(pooled) * gain).astype(bf16)
    scores = dot(emb, q_ref[:, :width], NT) * scale
    target = positive_row(q_ref, width)
    number = old_total + wide * 16 + core * 8 + lax.broadcasted_iota(i32, scores.shape, 0)
    top = jnp.max(scores, axis=0, keepdims=True)
    total = jnp.sum(jnp.exp(scores - top), axis=0, keepdims=True)
    picked = jnp.sum(jnp.where(number == target, scores, 0.0), axis=0, keepdims=True)
    olds = [get_stats(layer, width, count) for layer in layers]
    stats = merge(olds + [(top, total, picked)])
    out_ref[:, :width] = emb.astype(f32)
    put_stats(out_ref, width, stats)


def dispatch_kernel(where_ref, place_ref, mine_ref, other_ref, out_ref):
    width = mine_ref.shape[1] - 128
    count = (out_ref.shape[2] - width) // 3
    first = where_ref[1] == 0
    mine, other = mine_ref[:, :width], other_ref[:, :width]
    emb = jnp.concatenate([jnp.where(first, mine, other), jnp.where(first, other, mine)], axis=0)
    slots = dot(place_ref[:, :16], emb.astype(bf16), NN)
    top, total, picked = merge([get_stats(r[...], width, count) for r in (mine_ref, other_ref)])
    tails = [jnp.concatenate(split3(v), axis=1) for v in (top + jnp.log(total), picked)]
    for shard in range(16):
        for c in range(2):
            at = c * 16 + shard
            out_ref[shard, c : c + 1, :width] = slots[at : at + 1].astype(bf16)
            out_ref[shard, c : c + 1, width:] = tails[c]


def finish_kernel(where_ref, got_ref, index_ref, loss_ref):
    width = index_ref.shape[-1]
    count = (got_ref.shape[-1] - width) // 3
    narrow = where_ref[0] * 2 + where_ref[1]
    for source in range(2):
        index_ref[0, source] = got_ref[2 * narrow + source, :, :width]

    def whole(c):
        rows = [got_ref[w, c : c + 1, width:].astype(f32) for w in range(got_ref.shape[0])]
        rows = jnp.concatenate(rows, axis=0)
        high, middle, low = (rows[:, i * count : (i + 1) * count] for i in range(3))
        return (high + middle) + low

    parts, picks = whole(0), whole(1)
    top = jnp.max(parts, axis=0, keepdims=True)
    total = jnp.sum(jnp.exp(parts - top), axis=0, keepdims=True)
    loss = top + jnp.log(total) - jnp.sum(picks, axis=0, keepdims=True)
    lane = lax.broadcasted_iota(i32, (8, count), 1)
    sub = lax.broadcasted_iota(i32, (8, count), 0)
    masked = jnp.where((lane // 32) % 4 == sub, loss, 0.0)
    row = lax.broadcasted_iota(i32, (count, 128), 0)
    column = lax.broadcasted_iota(i32, (count, 128), 1)
    pick = (row // 128 == column // 32) & (row % 32 == column % 32)
    pick = jnp.where(pick, 1.0, 0.0).astype(bf16)
    high, middle, low = (dot(v, pick, NN) for v in split3(masked))
    loss_ref[...] = ((high + middle) + low)[0:4, 0:64]


def shift_z(value, k):
    return lax.ppermute(value, "narrow", [(i, i ^ (2 * k)) for i in range(8)])


def swap_core(value):
    return lax.ppermute(value, "narrow", [(i, i ^ 1) for i in range(8)])


def local(
    tokens,
    ln_gain,
    gate_weight,
    up_weight,
    down_weight,
    out_gain,
    shard_ids,
    slab_old,
    queries,
    positives,
    owners,
):
    width = tokens.shape[2]
    narrow, wide = lax.axis_index("narrow"), lax.axis_index("wide")
    z, core = (narrow >> 1).astype(i32), (narrow & 1).astype(i32)
    narrow_count, wide_count = lax.axis_size("narrow"), lax.axis_size("wide")
    old_total = slab_old.shape[0] * narrow_count * wide_count
    base = (wide * narrow_count + narrow) * slab_old.shape[0]
    where = jnp.stack([z, core, base, wide]).astype(i32)
    scale = 1.0 / math.sqrt(width)
    small = pltpu.CompilerParams(vmem_limit_bytes=16 << 20)
    steps = owners.shape[0]

    wg, wu = gate_weight.T, up_weight.T
    with jax.named_scope("query_wide"):
        got = front(core.reshape(1), queries, positives, wide_count)
        got = lax.all_to_all(got, "wide", split_axis=0, concat_axis=0, tiled=True)
    keep, send, place = encode(where, shard_ids, ln_gain, tokens, wg, wu, down_weight)
    with jax.named_scope("sum_core"):
        arrived = swap_core(send)
    own = pl.pallas_call(
        pick_kernel,
        in_specs=[SMEM, VMEM, ANY],
        out_specs=VMEM,
        out_shape=jax.ShapeDtypeStruct((steps * queries.shape[1] // 2, width + 128), bf16),
        cost_estimate=pl.CostEstimate(
            flops=PICK_FLOPS, transcendentals=0, bytes_accessed=got.size * 2
        ),
        compiler_params=small,
        name="pick",
    )(owners, got, keep)
    with jax.named_scope("query_core"):
        other = swap_core(own)

    stats, q = score(where, own, other, slab_old, scale)
    packed = jax.ShapeDtypeStruct((8, width + 128), f32)
    summed = pl.pallas_call(
        pack_kernel,
        in_specs=[VMEM] * 3,
        out_specs=VMEM,
        out_shape=packed,
        compiler_params=small,
        name="pack",
    )(keep, arrived, stats)
    with jax.named_scope("sum_z"):
        parts = [summed] + [shift_z(summed, k) for k in range(1, SIDE)]
    embedded = pl.pallas_call(
        functools.partial(embed_kernel, scale, old_total),
        in_specs=[SMEM] + [VMEM] * (2 + SIDE),
        out_specs=VMEM,
        out_shape=packed,
        scratch_shapes=[pltpu.VMEM((SIDE,) + packed.shape, f32)],
        compiler_params=small,
        name="embed",
    )(where, out_gain, q, *parts)
    with jax.named_scope("embed_core"):
        partner = swap_core(embedded)
    outgoing = pl.pallas_call(
        dispatch_kernel,
        in_specs=[SMEM] + [VMEM] * 3,
        out_specs=VMEM,
        out_shape=jax.ShapeDtypeStruct((16, 2, width + 3 * q.shape[0]), bf16),
        compiler_params=small,
        name="dispatch",
    )(where, place, embedded, partner)
    arrived = lax.all_to_all(outgoing, "wide", split_axis=0, concat_axis=0, tiled=True)
    return tuple(
        pl.pallas_call(
            finish_kernel,
            in_specs=[SMEM, VMEM],
            out_specs=[VMEM] * 2,
            out_shape=[
                jax.ShapeDtypeStruct((1, 2, 2, width), bf16),
                jax.ShapeDtypeStruct((steps, 64), f32),
            ],
            compiler_params=small,
        name="finish",
        )(where, arrived)
    )


def solution(mesh):
    return jax.shard_map(
        local,
        mesh=mesh,
        in_specs=(
            P("wide", None, None),
            P(),
            P(None, "narrow"),
            P(None, "narrow"),
            P("narrow", None),
            P(),
            P("wide"),
            P(("wide", "narrow"), None),
            P("wide", None, None),
            P("wide", None),
            P(),
        ),
        out_specs=(P("wide", "narrow", None, None), P()),
        check_vma=False,
    )
```

```python
import functools
import math

import jax
import jax.numpy as jnp
from jax import lax
from jax.experimental import pallas as pl
from jax.experimental.pallas import tpu as pltpu
from jax.sharding import PartitionSpec as P

EPS = 1e-06

f32, bf16, i32 = jnp.float32, jnp.bfloat16, jnp.int32
NT = (((1,), (1,)), ((), ()))
NN = (((1,), (0,)), ((), ()))
VMEM = pl.BlockSpec(memory_space=pltpu.VMEM)
SMEM = pl.BlockSpec(memory_space=pltpu.SMEM)
ANY = pl.BlockSpec(memory_space=pl.ANY)
HBM = pl.BlockSpec(memory_space=pltpu.HBM)

SCORE_BLOCK = 1024
FRONT_FLOPS = 10 * 10**9
PICK_FLOPS = 5 * 10**9
SIDE = 4
BLOCK = 4
HEAD = 3


def dot(a, b, dims):
    return lax.dot_general(a, b, dims, preferred_element_type=f32)


def split3(v):
    high = v.astype(bf16)
    rest = v - high.astype(f32)
    middle = rest.astype(bf16)
    low = (rest - middle.astype(f32)).astype(bf16)
    return high, middle, low


def rms_scale(values):
    return lax.rsqrt(jnp.mean(values * values, axis=-1, keepdims=True) + EPS)


def encode_kernel(
    where_ref,
    ids_ref,
    gain_ref,
    tok_hbm,
    wg_hbm,
    wu_hbm,
    down_hbm,
    keep_ref,
    send_ref,
    place_ref,
    hm_ref,
    tm_ref,
    tok_ref,
    w_ref,
    down_ref,
    tok_sem,
    w_sem,
    down_sem,
):
    blocks, count, units = hm_ref.shape
    seq, width = tok_hbm.shape[1:]
    tiles = w_ref.shape[0]
    gain = gain_ref[...].reshape(1, width).astype(f32)

    def fetch(b):
        slot = b % 2
        return pltpu.make_async_copy(
            tok_hbm.at[pl.ds(b * count, count)], tok_ref.at[slot], tok_sem.at[slot]
        )

    weights = []
    for j in range(tiles):
        size = min(128, units - 128 * j)
        for i, hbm in enumerate((wg_hbm, wu_hbm)):
            source = hbm.at[pl.ds(128 * j, size)]
            target = w_ref.at[j, pl.ds(128 * i, size)]
            weights.append(pltpu.make_async_copy(source, target, w_sem.at[j, i]))

    def block(b, wait):
        values = tok_ref[b % 2].reshape(count * seq, width).astype(f32)
        normed = (values * rms_scale(values) * gain).astype(bf16)
        tm_ref[b] = jnp.mean(values.reshape(count, seq, width), axis=1)
        for j in range(tiles):
            for before, after in wait.get(j, []):
                for copy in before:
                    copy.wait()
                for copy in after:
                    copy.start()
            out = dot(normed, w_ref[j], NT)
            gate, up = out[:, :128], out[:, 128:]
            hidden = (gate / (1.0 + jnp.exp(-gate)) * up).astype(bf16).astype(f32)
            mean = jnp.mean(hidden.reshape(count, seq, 128), axis=1)
            size = min(128, units - 128 * j)
            hm_ref[b, :, 128 * j : 128 * j + size] = mean[:, :size]

    fetch(0).start()
    early = weights[: 2 * HEAD]
    for copy in early:
        copy.start()
    fetch(0).wait()
    down = pltpu.make_async_copy(down_hbm, down_ref, down_sem)
    later = weights[2 * HEAD :]
    block(0, {0: [(early, later)], HEAD: [(later, [fetch(1), down])]})

    @pl.loop(1, blocks)
    def _(b):
        @pl.when(b + 1 < blocks)
        def _():
            fetch(b + 1).start()

        fetch(b).wait()
        block(b, {})

    down.wait()
    finish_pooled(where_ref, ids_ref, down_ref, hm_ref, tm_ref, keep_ref, send_ref, place_ref)


def encode(where, ids, gain, tokens, wg, wu, down):
    passages, seq, width = tokens.shape
    blocks = passages // BLOCK
    units = wg.shape[0]
    tiles = -(-units // 128)
    large = [pltpu.with_memory_space_constraint(v, pltpu.HBM) for v in (tokens, wg, wu, down)]
    half = jax.ShapeDtypeStruct((passages // 2, width), f32)
    return pl.pallas_call(
        encode_kernel,
        in_specs=[SMEM, VMEM, VMEM] + [HBM] * 4,
        out_specs=[VMEM] * 3,
        out_shape=[half, half, jax.ShapeDtypeStruct((32, 128), bf16)],
        scratch_shapes=[
            pltpu.VMEM((blocks, BLOCK, units), f32),
            pltpu.VMEM((blocks, BLOCK, width), f32),
            pltpu.VMEM((2, BLOCK, seq, width), bf16),
            pltpu.VMEM((tiles, 256, width), bf16),
            pltpu.VMEM(down.shape, bf16),
            pltpu.SemaphoreType.DMA((2,)),
            pltpu.SemaphoreType.DMA((tiles, 2)),
            pltpu.SemaphoreType.DMA,
        ],
        cost_estimate=pl.CostEstimate(
            flops=4 * passages * seq * width * units,
            transcendentals=passages * seq * units,
            bytes_accessed=2 * (passages * seq + 3 * units) * width,
        ),
        compiler_params=pltpu.CompilerParams(vmem_limit_bytes=28 << 20),
        name="encode",
    )(where, ids, gain, *large)


def finish_pooled(where_ref, ids_ref, down_ref, hm_ref, tm_ref, keep_ref, send_ref, place_ref):
    hm = jnp.concatenate([hm_ref[i] for i in range(hm_ref.shape[0])], axis=0)
    tm = jnp.concatenate([tm_ref[i] for i in range(tm_ref.shape[0])], axis=0)
    rows = hm.shape[0]
    parts = jnp.concatenate(split3(hm), axis=0)
    out = dot(parts, down_ref[...], NN)
    part = out[:rows] + (out[rows : 2 * rows] + out[2 * rows :])
    narrow = where_ref[0] * 2 + where_ref[1]
    row = lax.broadcasted_iota(i32, part.shape, 0)
    part = part + jnp.where(row // 2 == narrow, tm, 0.0)
    half = rows // 2
    low, high = part[:half], part[half:]
    first = where_ref[1] == 0
    keep_ref[...] = jnp.where(first, low, high)
    send_ref[...] = jnp.where(first, high, low)
    id_row = jnp.concatenate([ids_ref[...].reshape(1, rows), jnp.zeros((1, 128 - rows), i32)], axis=1)
    ids = jnp.broadcast_to(id_row, (128, 128)).astype(f32)
    column = jnp.transpose(ids)
    sub = lax.broadcasted_iota(i32, (128, 128), 0)
    lane = lax.broadcasted_iota(i32, (128, 128), 1)
    same = (ids == column) & (sub < lane) & (sub < rows)
    rank = jnp.sum(jnp.where(same, 1.0, 0.0), axis=0, keepdims=True)
    slot = lax.broadcasted_iota(i32, (32, 128), 0)
    ids32 = jnp.broadcast_to(id_row, (32, 128))
    hit = (ids32 == slot % 16) & (rank.astype(i32) == slot // 16)
    hit = hit & (lax.broadcasted_iota(i32, (32, 128), 1) < rows)
    place_ref[...] = jnp.where(hit, 1.0, 0.0).astype(bf16)


def front_kernel(core_ref, query_ref, positive_ref, out_ref):
    rows, width = query_ref.shape[1:]
    spare = out_ref.shape[1] - rows * width // 128
    first = core_ref[0] == 0
    number = jnp.where(first, positive_ref[:, :rows], positive_ref[:, rows:])
    number = jnp.concatenate([number, jnp.zeros((1, 128 - rows), i32)], axis=1)
    sub = lax.broadcasted_iota(i32, (spare, 128), 0)
    digits = jnp.where(sub == 0, number >> 16, jnp.where(sub == 1, (number >> 8) & 255, number & 255))
    digits = jnp.where(sub < 3, digits, 0).astype(f32).astype(bf16)
    for w in range(out_ref.shape[0]):
        for j in range(width // 128):
            out_ref[w, j * rows : (j + 1) * rows, :] = query_ref[0, :, j * 128 : (j + 1) * 128]
        out_ref[w, rows * width // 128 :, :] = digits


def front(core, queries, positives, copies):
    size, width = queries.shape[1:]
    rows = size // 2
    queries, positives = (
        pltpu.with_memory_space_constraint(v, pltpu.HBM) for v in (queries, positives)
    )
    shape = jax.ShapeDtypeStruct((copies, rows * width // 128 + 8, 128), bf16)
    return pl.pallas_call(
        front_kernel,
        grid_spec=pltpu.PrefetchScalarGridSpec(
            num_scalar_prefetch=1,
            grid=(1,),
            in_specs=[
                pl.BlockSpec((1, rows, width), lambda i, c: (0, c[0], 0)),
                pl.BlockSpec((1, size), lambda i, c: (0, 0)),
            ],
            out_specs=pl.BlockSpec(shape.shape, lambda i, c: (0, 0, 0)),
        ),
        out_shape=shape,
        cost_estimate=pl.CostEstimate(flops=FRONT_FLOPS, transcendentals=0, bytes_accessed=2 << 20),
        compiler_params=pltpu.CompilerParams(vmem_limit_bytes=8 << 20),
        name="front",
    )(core, queries, positives)


def pick_kernel(owners_ref, got_ref, after_ref, out_ref):
    width = out_ref.shape[1] - 128
    tiles = width // 128
    rows = (got_ref.shape[1] - 8) // tiles
    unit = lax.broadcasted_iota(i32, (rows, 128), 0) == lax.broadcasted_iota(i32, (rows, 128), 1)
    unit = jnp.where(unit, 1.0, 0.0).astype(bf16)
    for t in range(out_ref.shape[0] // rows):
        owner = owners_ref[t]
        at = slice(t * rows, (t + 1) * rows)
        for j in range(tiles):
            out_ref[at, j * 128 : (j + 1) * 128] = got_ref[owner, j * rows : (j + 1) * rows, :]
        digits = got_ref[owner, tiles * rows :, :].astype(f32)
        digits = jnp.concatenate([digits, jnp.zeros((120, 128), f32)], axis=0).astype(bf16)
        out_ref[at, width:] = dot(unit, digits, NT).astype(bf16)


def score_kernel(scale, where_ref, own_ref, other_ref, slab_hbm, stats_ref, q_ref, slab_ref, sem):
    chunks, block, width = slab_ref.shape
    half = own_ref.shape[0]
    copies = [
        pltpu.make_async_copy(slab_hbm.at[pl.ds(i * block, block)], slab_ref.at[i], sem.at[i])
        for i in range(chunks)
    ]
    copies[0].start()
    core = where_ref[1]
    q_ref[pl.ds(pl.multiple_of(core * half, half), half), :] = own_ref[...]
    q_ref[pl.ds(pl.multiple_of((1 - core) * half, half), half), :] = other_ref[...]
    target = positive_row(q_ref, width) - where_ref[2]
    found = []
    for i in range(chunks):
        copies[i].wait()
        if i == 0:
            for copy in copies[1:]:
                copy.start()
        for lo in range(0, block, 256):
            scores = dot(slab_ref[i, lo : lo + 256, :], q_ref[:, :width], NT) * scale
            row = lax.broadcasted_iota(i32, scores.shape, 0) + (i * block + lo)
            top = jnp.max(scores, axis=0, keepdims=True)
            total = jnp.sum(jnp.exp(scores - top), axis=0, keepdims=True)
            picked = jnp.sum(jnp.where(row == target, scores, 0.0), axis=0, keepdims=True)
            found.append((top, total, picked))
    stats_ref[...] = jnp.zeros(stats_ref.shape, f32)
    for i, value in enumerate(merge(found)):
        stats_ref[i : i + 1, :] = value


def positive_row(q_ref, width):
    lane = lax.broadcasted_iota(i32, (8, 128), 1)
    weight = jnp.where(lane == 0, 65536.0, jnp.where(lane == 1, 256.0, 1.0))
    weight = jnp.where(lane < 3, weight, 0.0).astype(bf16)
    return dot(weight, q_ref[:, width:], NT)[0:1].astype(i32)


def score(where, own, other, slab, scale):
    rows, width = slab.shape
    queries, lanes = 2 * own.shape[0], own.shape[1]
    return pl.pallas_call(
        functools.partial(score_kernel, scale),
        in_specs=[SMEM, VMEM, VMEM, HBM],
        out_specs=[VMEM] * 2,
        out_shape=[
            jax.ShapeDtypeStruct((8, queries), f32),
            jax.ShapeDtypeStruct((queries, lanes), bf16),
        ],
        scratch_shapes=[
            pltpu.VMEM((rows // SCORE_BLOCK, SCORE_BLOCK, width), bf16),
            pltpu.SemaphoreType.DMA((rows // SCORE_BLOCK,)),
        ],
        cost_estimate=pl.CostEstimate(
            flops=2 * rows * width * queries,
            transcendentals=rows * queries,
            bytes_accessed=2 * rows * width,
        ),
        compiler_params=pltpu.CompilerParams(vmem_limit_bytes=16 << 20),
        name="score",
    )(where, own, other, pltpu.with_memory_space_constraint(slab, pltpu.HBM))


def merge(parts):
    top = functools.reduce(jnp.maximum, [p[0] for p in parts])
    total = sum(p[1] * jnp.exp(p[0] - top) for p in parts)
    picked = sum(p[2] for p in parts)
    return top, total, picked


def stats_of(row, base, count):
    return tuple(row[:, base + i * count : base + (i + 1) * count] for i in range(3))


def put_stats(ref, width, stats):
    flat = jnp.concatenate(stats, axis=1)
    rows = flat.shape[1] // 128
    for i in range(ref.shape[0]):
        lanes = flat[:, i * 128 : (i + 1) * 128] if i < rows else jnp.zeros((1, 128), f32)
        ref[i : i + 1, width:] = lanes


def get_stats(value, width, count):
    flat = jnp.concatenate([value[i : i + 1, width:] for i in range(3 * count // 128)], axis=1)
    return stats_of(flat, 0, count)


def pack_kernel(keep_ref, got_ref, stats_ref, out_ref):
    width = keep_ref.shape[1]
    out_ref[:, :width] = keep_ref[...] + got_ref[...]
    put_stats(out_ref, width, [stats_ref[i : i + 1, :] for i in range(3)])


def embed_kernel(scale, old_total, where_ref, gain_ref, q_ref, *rest):
    ins, out_ref, layers_ref = rest[:SIDE], rest[SIDE], rest[SIDE + 1]
    width = gain_ref.shape[0]
    count = q_ref.shape[0]
    z, core, wide = where_ref[0], where_ref[1], where_ref[3]
    for k in range(SIDE):
        layers_ref[lax.bitwise_xor(z, k)] = ins[k][...]
    layers = [layers_ref[k] for k in range(SIDE)]
    pooled = (layers[0][:, :width] + layers[1][:, :width]) + (
        layers[2][:, :width] + layers[3][:, :width]
    )
    gain = gain_ref[...].reshape(1, width).astype(f32)
    emb = (pooled * rms_scale(pooled) * gain).astype(bf16)
    scores = dot(emb, q_ref[:, :width], NT) * scale
    target = positive_row(q_ref, width)
    number = old_total + wide * 16 + core * 8 + lax.broadcasted_iota(i32, scores.shape, 0)
    top = jnp.max(scores, axis=0, keepdims=True)
    total = jnp.sum(jnp.exp(scores - top), axis=0, keepdims=True)
    picked = jnp.sum(jnp.where(number == target, scores, 0.0), axis=0, keepdims=True)
    olds = [get_stats(layer, width, count) for layer in layers]
    stats = merge(olds + [(top, total, picked)])
    out_ref[:, :width] = emb.astype(f32)
    put_stats(out_ref, width, stats)


def dispatch_kernel(where_ref, place_ref, mine_ref, other_ref, out_ref):
    width = mine_ref.shape[1] - 128
    count = (out_ref.shape[2] - width) // 3
    first = where_ref[1] == 0
    mine, other = mine_ref[:, :width], other_ref[:, :width]
    emb = jnp.concatenate([jnp.where(first, mine, other), jnp.where(first, other, mine)], axis=0)
    slots = dot(place_ref[:, :16], emb.astype(bf16), NN)
    top, total, picked = merge([get_stats(r[...], width, count) for r in (mine_ref, other_ref)])
    tails = [jnp.concatenate(split3(v), axis=1) for v in (top + jnp.log(total), picked)]
    for shard in range(16):
        for c in range(2):
            at = c * 16 + shard
            out_ref[shard, c : c + 1, :width] = slots[at : at + 1].astype(bf16)
            out_ref[shard, c : c + 1, width:] = tails[c]


def finish_kernel(where_ref, got_ref, index_ref, loss_ref):
    width = index_ref.shape[-1]
    count = (got_ref.shape[-1] - width) // 3
    narrow = where_ref[0] * 2 + where_ref[1]
    for source in range(2):
        index_ref[0, source] = got_ref[2 * narrow + source, :, :width]

    def whole(c):
        rows = [got_ref[w, c : c + 1, width:].astype(f32) for w in range(got_ref.shape[0])]
        rows = jnp.concatenate(rows, axis=0)
        high, middle, low = (rows[:, i * count : (i + 1) * count] for i in range(3))
        return (high + middle) + low

    parts, picks = whole(0), whole(1)
    top = jnp.max(parts, axis=0, keepdims=True)
    total = jnp.sum(jnp.exp(parts - top), axis=0, keepdims=True)
    loss = top + jnp.log(total) - jnp.sum(picks, axis=0, keepdims=True)
    lane = lax.broadcasted_iota(i32, (8, count), 1)
    sub = lax.broadcasted_iota(i32, (8, count), 0)
    masked = jnp.where((lane // 32) % 4 == sub, loss, 0.0)
    row = lax.broadcasted_iota(i32, (count, 128), 0)
    column = lax.broadcasted_iota(i32, (count, 128), 1)
    pick = (row // 128 == column // 32) & (row % 32 == column % 32)
    pick = jnp.where(pick, 1.0, 0.0).astype(bf16)
    high, middle, low = (dot(v, pick, NN) for v in split3(masked))
    loss_ref[...] = ((high + middle) + low)[0:4, 0:64]


def shift_z(value, k):
    return lax.ppermute(value, "narrow", [(i, i ^ (2 * k)) for i in range(8)])


def swap_core(value):
    return lax.ppermute(value, "narrow", [(i, i ^ 1) for i in range(8)])


def local(
    tokens,
    ln_gain,
    gate_weight,
    up_weight,
    down_weight,
    out_gain,
    shard_ids,
    slab_old,
    queries,
    positives,
    owners,
):
    width = tokens.shape[2]
    narrow, wide = lax.axis_index("narrow"), lax.axis_index("wide")
    z, core = (narrow >> 1).astype(i32), (narrow & 1).astype(i32)
    narrow_count, wide_count = lax.axis_size("narrow"), lax.axis_size("wide")
    old_total = slab_old.shape[0] * narrow_count * wide_count
    base = (wide * narrow_count + narrow) * slab_old.shape[0]
    where = jnp.stack([z, core, base, wide]).astype(i32)
    scale = 1.0 / math.sqrt(width)
    small = pltpu.CompilerParams(vmem_limit_bytes=16 << 20)
    steps = owners.shape[0]

    wg, wu = gate_weight.T, up_weight.T
    with jax.named_scope("query_wide"):
        got = front(core.reshape(1), queries, positives, wide_count)
        got = lax.all_to_all(got, "wide", split_axis=0, concat_axis=0, tiled=True)
    keep, send, place = encode(where, shard_ids, ln_gain, tokens, wg, wu, down_weight)
    with jax.named_scope("sum_core"):
        arrived = swap_core(send)
    own = pl.pallas_call(
        pick_kernel,
        in_specs=[SMEM, VMEM, ANY],
        out_specs=VMEM,
        out_shape=jax.ShapeDtypeStruct((steps * queries.shape[1] // 2, width + 128), bf16),
        cost_estimate=pl.CostEstimate(
            flops=PICK_FLOPS, transcendentals=0, bytes_accessed=got.size * 2
        ),
        compiler_params=small,
        name="pick",
    )(owners, got, keep)
    with jax.named_scope("query_core"):
        other = swap_core(own)

    stats, q = score(where, own, other, slab_old, scale)
    packed = jax.ShapeDtypeStruct((8, width + 128), f32)
    summed = pl.pallas_call(
        pack_kernel,
        in_specs=[VMEM] * 3,
        out_specs=VMEM,
        out_shape=packed,
        compiler_params=small,
        name="pack",
    )(keep, arrived, stats)
    with jax.named_scope("sum_z"):
        parts = [summed] + [shift_z(summed, k) for k in range(1, SIDE)]
    embedded = pl.pallas_call(
        functools.partial(embed_kernel, scale, old_total),
        in_specs=[SMEM] + [VMEM] * (2 + SIDE),
        out_specs=VMEM,
        out_shape=packed,
        scratch_shapes=[pltpu.VMEM((SIDE,) + packed.shape, f32)],
        compiler_params=small,
        name="embed",
    )(where, out_gain, q, *parts)
    with jax.named_scope("embed_core"):
        partner = swap_core(embedded)
    outgoing = pl.pallas_call(
        dispatch_kernel,
        in_specs=[SMEM] + [VMEM] * 3,
        out_specs=VMEM,
        out_shape=jax.ShapeDtypeStruct((16, 2, width + 3 * q.shape[0]), bf16),
        compiler_params=small,
        name="dispatch",
    )(where, place, embedded, partner)
    arrived = lax.all_to_all(outgoing, "wide", split_axis=0, concat_axis=0, tiled=True)
    return tuple(
        pl.pallas_call(
            finish_kernel,
            in_specs=[SMEM, VMEM],
            out_specs=[VMEM] * 2,
            out_shape=[
                jax.ShapeDtypeStruct((1, 2, 2, width), bf16),
                jax.ShapeDtypeStruct((steps, 64), f32),
            ],
            compiler_params=small,
        name="finish",
        )(where, arrived)
    )


def solution(mesh):
    return jax.shard_map(
        local,
        mesh=mesh,
        in_specs=(
            P("wide", None, None),
            P(),
            P(None, "narrow"),
            P(None, "narrow"),
            P("narrow", None),
            P(),
            P("wide"),
            P(("wide", "narrow"), None),
            P("wide", None, None),
            P("wide", None),
            P(),
        ),
        out_specs=(P("wide", "narrow", None, None), P()),
        check_vma=False,
    )
```
